32 devices in a mesh: dp: 8 (over y, x, core), seq: 4 (over z).
Axes of the slice: x: 2, y: 2, z: 4, core: 2. Of those that a mesh axis runs over, the one named last changes fastest.
Arguments:
- tokens: bfloat16 [8, 2048, 768], P('dp', 'seq'), may hold values from -6 to 6
- segment_ids: int32 [8, 2048], P('dp'), may hold values from 0 to 3, never falling along the last dimension, each value on 1 to 1024 neighbouring positions
- first_gain: float32 [768], replicated, may hold values from 0.5 to 1.5
- qkv_weight: bfloat16 [768, 2304], replicated, may hold values from -0.21875 to 0.21875
- out_weight: bfloat16 [768, 768], replicated, may hold values from -1.25 to 1.25
- second_gain: float32 [768], replicated, may hold values from 0.5 to 1.5
- in_weight: bfloat16 [768, 2304], replicated, may hold values from -0.21875 to 0.21875
- down_weight: bfloat16 [1152, 768], replicated, may hold values from -0.1875 to 0.1875
- cotangent: bfloat16 [8, 2048, 768], P('dp', 'seq'), may hold values from -6 to 6
Outputs:
- output: bfloat16 [8, 2048, 768], P('dp', 'seq')
- input_grad: bfloat16 [8, 2048, 768], P('dp', 'seq')
- qkv_weight_grad: float32 [768, 2304], P('seq')
- out_weight_grad: float32 [768, 768], P('seq')
- in_weight_grad: float32 [768, 2304], P('seq')
- down_weight_grad: float32 [1152, 768], P('seq')
- first_gain_grad: float32 [768], P('seq')
- second_gain_grad: float32 [768], P('seq')
The draws below stay inside these ranges and needn't reach their ends.
Inputs may be any that keep to these rules, and one draw needn't show every extreme that they name: `segment_ids`: within a row the ids never fall; a document is a run of equal ids of 1 to 1024 tokens.
All inputs are finite; a program needn't handle non-finite values.
Results may differ from the reference program's by a relative error of at most 0.014.
Values may be sent and summed in bfloat16 or wider, within the bound.
No kernel may reach another device: no remote copies, remote signals or barrier semaphores. Data moves between devices by JAX's collectives and lax.ppermute only.
A program may use at most 192 MiB of HBM per device.

```python
import math
import jax
import jax.numpy as jnp
import numpy as np
from jax import lax

D = 768
HEADS = 12
HEAD_DIM = 64
FF = 1152
DOCS = 4
ROW = 2048
ROWS = 8


def shard_levels(rng, extent, cuts, least, top_value):
    def one(axis_at, shards_of):
        draws = jax.random.uniform(jax.random.fold_in(jax.random.fold_in(rng, 6), axis_at), (shards_of,), jnp.float32, least / len(cuts), top_value / len(cuts))
        return jnp.repeat(jnp.exp(draws), extent[axis_at] // shards_of).reshape((-1,) + (1,) * (len(extent) - axis_at - 1))

    factor_of = one(*cuts[0])
    for cut in cuts[1:]:
        factor_of = factor_of * one(*cut)
    return factor_of


def profile(amount, total, bound, lean):
    portions = [(1 << 20) // math.isqrt(rank ** lean) + 1 for rank in range(2, amount + 1)]
    rest, counts = total - bound - (amount - 1), [1] * (amount - 1)
    while rest > 0:
        candidates = [i for i in range(amount - 1) if counts[i] < bound]
        pool, budget = sum([portions[i] for i in candidates]), rest
        for i in candidates:
            more = min(bound - counts[i], max(1, budget * portions[i] // pool), rest)
            counts[i] = counts[i] + more
            rest = rest - more
    return np.array([bound] + counts)


def ragged(key, number_of, total, bound, skew):
    if number_of == 2:
        one = jax.random.randint(key, (), max(1, total - bound), min(bound, total - 1) + 1)
        return jnp.stack([one, total - one])
    sizes = jnp.asarray(profile(number_of, total, bound, skew), jnp.int32)
    pairs = (number_of - 1) // 2
    donor, sink = sizes[1:1 + 2 * pairs:2], sizes[2:2 + 2 * pairs:2]
    slack = jnp.minimum(donor - 1, bound - sink)
    passed = jax.random.randint(jax.random.fold_in(key, 1), (pairs,), 0, 1 << 20) % (slack + 1)
    sizes = sizes.at[1:1 + 2 * pairs:2].set(donor - passed).at[2:2 + 2 * pairs:2].set(sink + passed)
    return sizes[jax.random.permutation(jax.random.fold_in(key, 2), number_of)]


def gaussian(rng, extent, spread, bound, split=(), kind=jnp.bfloat16):
    factor_of = shard_levels(rng, extent, split, -0.22, 0.18) if split else 1.0
    drawn = jax.random.normal(rng, extent, jnp.float32) * spread * factor_of
    return jnp.minimum(jnp.maximum(drawn, -bound), bound).astype(kind)


def setup_inputs(seed: int = 0) -> dict:
    streams_of = jax.random.split(jax.random.key(seed), 10)
    return {
        "tokens": gaussian(streams_of[0], (ROWS, ROW, D), 1.0, 6.0, ((0, 8), (1, 4))),
        "segment_ids": jax.vmap(lambda own: jnp.searchsorted(jnp.cumsum(ragged(own, DOCS, ROW, ROW // 2, 2)), jnp.arange(ROW), side="right"))(jax.random.split(streams_of[1], ROWS)).reshape((ROWS, ROW)).astype(jnp.int32),
        "first_gain": jnp.clip(1.0 + 0.1 * jax.random.normal(streams_of[2], (D,), jnp.float32), 0.5, 1.5),
        "qkv_weight": gaussian(streams_of[3], (D, 3 * D), D ** -0.5, 0.21875),
        "out_weight": gaussian(streams_of[4], (D, D), (D // 32) ** -0.5, 1.25),
        "second_gain": jnp.clip(1.0 + 0.1 * jax.random.normal(streams_of[5], (D,), jnp.float32), 0.5, 1.5),
        "in_weight": gaussian(streams_of[6], (D, 2 * FF), D ** -0.5, 0.21875),
        "down_weight": gaussian(streams_of[7], (FF, D), FF ** -0.5, 0.1875),
        "cotangent": gaussian(streams_of[8], (ROWS, ROW, D), 1.0, 6.0, ((0, 8), (1, 4))),
    }


epsilon = 1e-05
rope_base = 160000.0
highest = lax.Precision.HIGHEST

@jax.custom_vjp
def low(v):
    return lax.optimization_barrier(v.astype(jnp.bfloat16)).astype(jnp.float32)

@jax.custom_vjp
def low_back(v):
    return v

def low_keep(v):
    return (low(v), None)

def low_pass(kept, grad):
    return (grad,)

def back_keep(v):
    return (v, None)

def back_low(kept, grad):
    return (low(grad),)
low.defvjp(low_keep, low_pass)
low_back.defvjp(back_keep, back_low)

def normalize(values):
    centred = values - lax.optimization_barrier(jnp.mean(values, axis=-1, keepdims=True))
    return centred * lax.rsqrt(lax.optimization_barrier(jnp.mean(centred * centred, axis=-1, keepdims=True)) + epsilon)

def rotary_tables(segments, head_dim):
    length = segments.shape[0]
    places = jnp.arange(length, dtype=jnp.int32)
    starts_flag = jnp.concatenate([jnp.ones((1,), jnp.bool_), segments[1:] != segments[:-1]])
    starts = lax.cummax(jnp.where(starts_flag, places, jnp.zeros_like(places)), axis=0)
    offsets = (places - starts).astype(jnp.float32)
    freqs = jnp.exp(jnp.arange(head_dim // 2, dtype=jnp.float32) * (-2.0 * math.log(rope_base) / head_dim))
    angles = offsets[:, None] * freqs[None, :]
    angles = jnp.concatenate([angles, angles], axis=1)
    return (jnp.cos(angles), jnp.sin(angles))

def rotate(values, cosine, sine):
    half_dim = values.shape[-1] // 2
    turned = jnp.concatenate([-values[..., half_dim:], values[..., :half_dim]], axis=-1)
    return values * cosine + turned * sine

def attention(query_rows, key_rows, value_rows, segments):
    inv_root = 1.0 / math.sqrt(query_rows.shape[-1])
    raw_scores = jnp.einsum('qhd,khd->hqk', query_rows, key_rows, precision=highest) * inv_root
    raw_scores = low_back(raw_scores)
    same_doc = (segments[:, None] == segments[None, :])[None]
    scores = jnp.where(same_doc, raw_scores, -1e+30)
    row_top = lax.optimization_barrier(jnp.max(scores, axis=-1, keepdims=True))
    exponent = jnp.exp(scores - row_top)
    soft_weights = low(exponent / lax.optimization_barrier(jnp.sum(exponent, axis=-1, keepdims=True)))
    return jnp.einsum('hqk,khd->qhd', soft_weights, value_rows, precision=highest)

def block_forward(inputs, gain_one, qkv_w, out_w, gain_two, in_w, down_w, segments, cosine, sine):
    length = inputs.shape[0]
    lowered_first = low(normalize(inputs) * gain_one)
    packed = low(low_back(jnp.dot(lowered_first, qkv_w, precision=highest)))
    split_rows = packed.reshape(length, 3, HEADS, HEAD_DIM)
    query_rows = low(rotate(split_rows[:, 0], cosine[:, None], sine[:, None]))
    key_rows = low(rotate(split_rows[:, 1], cosine[:, None], sine[:, None]))
    attended = jax.checkpoint(attention)(query_rows, key_rows, split_rows[:, 2], segments)
    context = low(low_back(attended.reshape(length, HEADS * HEAD_DIM)))
    residual = inputs + low_back(jnp.dot(context, out_w, precision=highest))
    lowered_second = low(normalize(residual) * gain_two)
    gate_up = low_back(jnp.dot(lowered_second, in_w, precision=highest))
    hidden = low(jax.nn.gelu(gate_up[:, :FF], approximate=False) * gate_up[:, FF:])
    return residual + jnp.dot(hidden, down_w, precision=highest)

def reference(tokens, segment_ids, first_gain, qkv_weight, out_weight, second_gain, in_weight, down_weight, cotangent):
    params = (first_gain, qkv_weight.astype(jnp.float32), out_weight.astype(jnp.float32), second_gain, in_weight.astype(jnp.float32), down_weight.astype(jnp.float32))

    def row_step(totals, blocks):
        row_tokens, row_segments, row_cot = blocks
        cosine, sine = rotary_tables(row_segments, HEAD_DIM)

        def forward(inputs, gain_one, qkv_w, out_w, gain_two, in_w, down_w):
            return block_forward(inputs, gain_one, qkv_w, out_w, gain_two, in_w, down_w, row_segments, cosine, sine)
        result, pullback = jax.vjp(forward, row_tokens.astype(jnp.float32), params[0], params[1], params[2], params[3], params[4], params[5])
        grads = pullback(row_cot.astype(jnp.float32))
        new_totals = tuple((totals[index] + grads[index + 1] for index in range(6)))
        return (new_totals, (result.astype(jnp.bfloat16), grads[0].astype(jnp.bfloat16)))
    init = tuple((jnp.zeros(weight.shape, jnp.float32) for weight in params))
    totals, outs_pair = lax.scan(row_step, init, (tokens, segment_ids, cotangent))
    return (outs_pair[0], outs_pair[1], totals[1], totals[2], totals[4], totals[5], totals[0], totals[3])
```

```python
import functools
import math

import jax
import jax.numpy as jnp
from jax import lax
from jax.experimental import pallas as pl
from jax.experimental.pallas import tpu as pltpu
from jax.sharding import PartitionSpec as P

HEAD_DIM = 64
DOCS = 4
LONGEST = 1024
CHUNK = 256
LANES = 128

epsilon = 1e-05
rope_base = 160000.0
f32 = jnp.float32
bf16 = jnp.bfloat16
MIB = 1 << 20


def dot_nn(a, b):
    return lax.dot_general(a, b, (((1,), (0,)), ((), ())), preferred_element_type=f32)


def dot_nt(a, b):
    return lax.dot_general(a, b, (((1,), (1,)), ((), ())), preferred_element_type=f32)


def normalize(values):
    centred = values - jnp.mean(values, axis=-1, keepdims=True)
    inv_scale = lax.rsqrt(jnp.mean(centred * centred, axis=-1, keepdims=True) + epsilon)
    return (centred * inv_scale, inv_scale)


def normalize_back(grad_normed, normed, inv_scale):
    return inv_scale * (
        grad_normed
        - jnp.mean(grad_normed, axis=-1, keepdims=True)
        - normed * jnp.mean(grad_normed * normed, axis=-1, keepdims=True)
    )


def partner(values):
    lane = lax.broadcasted_iota(jnp.int32, values.shape, 1) % HEAD_DIM
    return jnp.where(
        lane < HEAD_DIM // 2,
        pltpu.roll(values, LANES - HEAD_DIM // 2, 1),
        pltpu.roll(values, HEAD_DIM // 2, 1),
    )


def project_kernel(
    bounds, x_ref, gain_ref, w_ref, cos_ref, sin_ref, *refs, own, first, last_bound
):
    outs = refs if own else refs[5:]
    low_ref, low_t_ref, k_ref, k_t_ref, v_ref = outs[:5]
    rows, width = x_ref.shape
    pairs = width // LANES

    def one(at):
        here = pl.ds(at * CHUNK, CHUNK)
        normed, _ = normalize(x_ref[here, :].astype(f32))
        low = (normed * gain_ref[...]).astype(bf16)
        low_ref[here, :] = low
        low_t_ref[:, here] = low.T
        cosine, sine = cos_ref[here, :], sin_ref[here, :]

        def rotated(start, scale, plain_ref, turned_ref):
            packed = dot_nn(low, w_ref[:, start : start + width]).astype(bf16).astype(f32)
            for pair in range(pairs):
                lanes = slice(pair * LANES, (pair + 1) * LANES)
                part = packed[:, lanes]
                part = ((part * cosine + partner(part) * sine).astype(bf16) * scale).astype(bf16)
                plain_ref[here, lanes] = part
                turned_ref[lanes, here] = part.T

        if own:
            rotated(0, HEAD_DIM**-0.5, outs[5], outs[6])
        rotated(width, 1.0, k_ref, k_t_ref)
        v_ref[here, :] = dot_nn(low, w_ref[:, 2 * width :]).astype(bf16)

    for at in range(rows // CHUNK):
        if own:
            one(at)
        else:
            chunk = first + at
            pl.when((chunk >= bounds[0]) & (chunk < bounds[last_bound]))(
                functools.partial(one, at)
            )


def project(bounds, x, gain, weight, cosine, sine, block, blocks, held=None):
    rows, width = x.shape
    whole = rows * blocks
    own = held is None
    by_rows = pl.BlockSpec((rows, width), lambda i: (block, 0))
    by_lanes = pl.BlockSpec((width, rows), lambda i: (0, block))
    table = pl.BlockSpec((rows, LANES), lambda i: (block, 0))
    tall = jax.ShapeDtypeStruct((whole, width), bf16)
    wide = jax.ShapeDtypeStruct((width, whole), bf16)
    out_shape = [tall, wide, tall, wide, tall]
    out_specs = [by_rows, by_lanes, by_rows, by_lanes, by_rows]
    if own:
        out_shape += [
            jax.ShapeDtypeStruct((rows, width), bf16),
            jax.ShapeDtypeStruct((width, rows), bf16),
        ]
        out_specs += [
            pl.BlockSpec((rows, width), lambda i: (0, 0)),
            pl.BlockSpec((width, rows), lambda i: (0, 0)),
        ]
    parts = 3 if own else 2
    return pl.pallas_call(
        functools.partial(
            project_kernel,
            own=own,
            first=block * (rows // CHUNK),
            last_bound=bounds.shape[0] - 1,
        ),
        grid=(1,),
        out_shape=out_shape,
        in_specs=[
            pl.BlockSpec(memory_space=pltpu.SMEM),
            pl.BlockSpec((rows, width), lambda i: (0, 0)),
            pl.BlockSpec((1, width), lambda i: (0, 0)),
            pl.BlockSpec(weight.shape, lambda i: (0, 0)),
            table,
            table,
        ]
        + [pl.BlockSpec(memory_space=pl.ANY)] * (0 if own else 5),
        out_specs=out_specs,
        input_output_aliases={} if own else {6 + i: i for i in range(5)},
        compiler_params=pltpu.CompilerParams(vmem_limit_bytes=32 * MIB),
        cost_estimate=pl.CostEstimate(
            flops=2 * rows * width * width * parts,
            bytes_accessed=2 * (weight.size + rows * width * 7),
            transcendentals=rows,
        ),
        name=f"project_{block}",
    )(bounds, x, gain, weight, cosine, sine, *(held or ()))


def attend_kernel(
    bounds, q_ref, k_ref, v_ref, qseg_ref, kseg_ref, out_ref, lse_ref, bias, held, qm, top, total, acc
):
    rows, width = q_ref.shape
    group = 2 * LANES
    low_half = lax.broadcasted_iota(jnp.int32, (CHUNK, LANES), 1) < HEAD_DIM
    lane = lax.broadcasted_iota(jnp.int32, (CHUNK, LANES), 1)
    heads = range(group // HEAD_DIM)

    for block in range(rows // CHUNK):
        here = pl.ds(block * CHUNK, CHUNK)
        first, last = bounds[2 * block], bounds[2 * block + 1]

        @pl.loop(first, last)
        def _(c):
            bias[c] = jnp.where(qseg_ref[here, :] == kseg_ref[c], 0.0, -1e30)

        def one_group(g, logs):
            lanes = pl.ds(pl.multiple_of(g * group, group), group)
            q4 = q_ref[here, lanes]
            for h in heads:
                half = low_half if h % 2 == 0 else ~low_half
                q2 = q4[:, (h // 2) * LANES : (h // 2 + 1) * LANES]
                qm[h] = jnp.where(half, q2, jnp.zeros_like(q2))
                top[h] = jnp.full((CHUNK, LANES), -1e30, f32)
                total[h] = jnp.zeros((CHUNK, LANES), f32)
                acc[h] = jnp.zeros((CHUNK, LANES), f32)

            @pl.loop(first, last)
            def _(c):
                k4 = k_ref[pl.ds(pl.multiple_of(c * CHUNK, CHUNK), CHUNK), lanes]
                for h in heads:
                    k2 = k4[:, (h // 2) * LANES : (h // 2 + 1) * LANES]
                    s = dot_nt(qm[h], k2) + bias[c]
                    held[h, c] = s
                    top[h] = jnp.maximum(top[h], jnp.maximum(s[:, :LANES], s[:, LANES:]))

            for h in heads:
                top[h] = jnp.broadcast_to(jnp.max(top[h], axis=1, keepdims=True), (CHUNK, LANES))

            @pl.loop(first, last)
            def _(c):
                v4 = v_ref[pl.ds(pl.multiple_of(c * CHUNK, CHUNK), CHUNK), lanes]
                for h in heads:
                    v2 = v4[:, (h // 2) * LANES : (h // 2 + 1) * LANES]
                    s = held[h, c]
                    left = jnp.exp(s[:, :LANES] - top[h])
                    right = jnp.exp(s[:, LANES:] - top[h])
                    total[h] = total[h] + (left + right)
                    p = jnp.concatenate([left.astype(bf16), right.astype(bf16)], axis=1)
                    acc[h] = acc[h] + dot_nn(p, v2)

            outs = []
            for h in heads:
                row_total = jnp.sum(total[h], axis=1, keepdims=True)
                outs.append(acc[h] / row_total)
                logs = jnp.where(lane == g * len(heads) + h, top[h] + jnp.log(row_total), logs)
            for pair in range(len(heads) // 2):
                at = pl.ds(pl.multiple_of(g * group + pair * LANES, LANES), LANES)
                out_ref[here, at] = jnp.where(low_half, outs[2 * pair], outs[2 * pair + 1]).astype(bf16)
            return logs

        logs = lax.fori_loop(0, width // group, one_group, jnp.zeros((CHUNK, LANES), f32))
        lse_ref[:, here] = logs.T


def attend(bounds, q, k, v, qseg, kseg):
    rows, width = q.shape
    chunks = k.shape[0] // CHUNK
    heads = 2 * LANES // HEAD_DIM
    spec = pl.BlockSpec(memory_space=pltpu.VMEM)
    tile = pltpu.VMEM((heads, CHUNK, LANES), f32)
    return pl.pallas_call(
        attend_kernel,
        out_shape=[
            jax.ShapeDtypeStruct((rows, width), bf16),
            jax.ShapeDtypeStruct((LANES, rows), f32),
        ],
        in_specs=[pl.BlockSpec(memory_space=pltpu.SMEM)] + [spec] * 5,
        out_specs=[spec] * 2,
        scratch_shapes=[
            pltpu.VMEM((chunks, CHUNK, CHUNK), f32),
            pltpu.VMEM((heads, chunks, CHUNK, CHUNK), f32),
            pltpu.VMEM((heads, CHUNK, LANES), bf16),
            tile,
            tile,
            tile,
        ],
        compiler_params=pltpu.CompilerParams(vmem_limit_bytes=40 * MIB),
        cost_estimate=pl.CostEstimate(
            flops=4 * rows * LONGEST * width,
            bytes_accessed=2 * 2 * (rows + 2 * LONGEST) * width,
            transcendentals=rows * LONGEST * width // HEAD_DIM,
        ),
        name="attend",
    )(bounds, q, k, v, qseg, kseg)


def attend_back_kernel(
    bounds,
    q_ref,
    q_t_ref,
    k_ref,
    k_t_ref,
    v_ref,
    g_ref,
    out_ref,
    lse_ref,
    span_ref,
    cos_ref,
    sin_ref,
    dq_ref,
    dk_ref,
    dv_ref,
    qm,
    gm,
    delta,
    bias,
    dq_acc,
    dk_acc,
    dv_acc,
    *,
    own_at,
):
    rows, width = q_ref.shape
    blocks, pairs = rows // CHUNK, width // LANES
    group = 2 * LANES
    heads = range(group // HEAD_DIM)
    low_rows = lax.broadcasted_iota(jnp.int32, (LANES, rows), 0) < HEAD_DIM
    low_half = lax.broadcasted_iota(jnp.int32, (CHUNK, LANES), 1) < HEAD_DIM
    place = lax.broadcasted_iota(jnp.int32, (CHUNK, CHUNK), 0)

    def halves(parts):
        return jnp.concatenate(
            [jnp.where(low_half, parts[i], parts[i + 1]) for i in range(0, len(parts), 2)], axis=1
        )

    for pair in range(pairs):
        lanes = slice(pair * LANES, (pair + 1) * LANES)
        turned = q_t_ref[lanes, :]
        grad = g_ref[:, lanes].astype(f32).T
        both = grad * out_ref[:, lanes].astype(f32).T
        grad = grad.astype(bf16)
        for half in range(2):
            keep = low_rows if half == 0 else ~low_rows
            head = 2 * pair + half
            qm[head] = jnp.where(keep, turned, jnp.zeros_like(turned))
            gm[head] = jnp.where(keep, grad, jnp.zeros_like(grad))
            delta[head] = jnp.sum(
                both[half * HEAD_DIM : (half + 1) * HEAD_DIM, :], axis=0, keepdims=True
            )

    dq_acc[...] = jnp.zeros_like(dq_acc)

    @pl.loop(bounds[0], bounds[2 * blocks - 1])
    def _(c):
        keys = pl.ds(pl.multiple_of(c * CHUNK, CHUNK), CHUNK)
        dk_acc[keys, :] = jnp.zeros((CHUNK, width), f32)
        dv_acc[keys, :] = jnp.zeros((CHUNK, width), f32)

    for block in range(blocks):
        here = slice(block * CHUNK, (block + 1) * CHUNK)

        @pl.loop(bounds[2 * block], bounds[2 * block + 1])
        def _(c):
            keys = pl.ds(pl.multiple_of(c * CHUNK, CHUNK), CHUNK)
            at = place + c * CHUNK
            bias[...] = jnp.where(
                (at >= span_ref[0:1, here]) & (at < span_ref[1:2, here]), 0.0, -1e30
            )

            @pl.loop(0, width // group)
            def _(g):
                lanes = pl.ds(pl.multiple_of(g * group, group), group)
                k4, v4 = k_ref[keys, lanes], v_ref[keys, lanes]
                q4, g4 = q_ref[here, lanes], g_ref[here, lanes]
                turned = k_t_ref[lanes, keys]
                dks, dvs, dqs = [], [], []
                for h in heads:
                    two = slice((h // 2) * LANES, (h // 2 + 1) * LANES)
                    head = g * len(heads) + h
                    s = dot_nn(k4[:, two], qm[head, :, here])
                    p = jnp.exp((s + bias[...]) - lse_ref[head, :, here])
                    dp = dot_nn(v4[:, two], gm[head, :, here])
                    ds = (p * (dp - delta[head, :, here])).astype(bf16)
                    dvs.append(dot_nn(p.astype(bf16), g4[:, two]))
                    dks.append(dot_nn(ds, q4[:, two]))
                    dqs.append(dot_nn(turned[h * HEAD_DIM : (h + 1) * HEAD_DIM, :], ds))
                dq_acc[lanes, here] += jnp.concatenate(dqs, axis=0)
                dk_acc[keys, lanes] += halves(dks)
                dv_acc[keys, lanes] += halves(dvs)

    @pl.loop(bounds[0], bounds[2 * blocks - 1])
    def _(c):
        keys = pl.ds(pl.multiple_of(c * CHUNK, CHUNK), CHUNK)
        cosine, sine = cos_ref[keys, :], sin_ref[keys, :]
        for pair in range(pairs):
            lanes = slice(pair * LANES, (pair + 1) * LANES)
            part = dk_acc[keys, lanes]
            dk_ref[keys, lanes] = (part * cosine - partner(part) * sine).astype(bf16)
            dv_ref[keys, lanes] = dv_acc[keys, lanes].astype(bf16)

    cosine, sine = cos_ref[own_at : own_at + rows, :], sin_ref[own_at : own_at + rows, :]
    for pair in range(pairs):
        lanes = slice(pair * LANES, (pair + 1) * LANES)
        part = dq_acc[lanes, :].T * HEAD_DIM**-0.5
        dq_ref[:, lanes] = (part * cosine - partner(part) * sine).astype(bf16)


def attend_back(bounds, q, q_t, k, k_t, v, grad, context, lse, span, cosine, sine, own_at):
    rows, width = q.shape
    whole = k.shape[0]
    heads = width // HEAD_DIM
    spec = pl.BlockSpec(memory_space=pltpu.VMEM)
    return pl.pallas_call(
        functools.partial(attend_back_kernel, own_at=own_at),
        out_shape=[
            jax.ShapeDtypeStruct((rows, width), bf16),
            jax.ShapeDtypeStruct((whole, width), bf16),
            jax.ShapeDtypeStruct((whole, width), bf16),
        ],
        in_specs=[pl.BlockSpec(memory_space=pltpu.SMEM)] + [spec] * 11,
        out_specs=[spec] * 3,
        scratch_shapes=[
            pltpu.VMEM((heads, LANES, rows), bf16),
            pltpu.VMEM((heads, LANES, rows), bf16),
            pltpu.VMEM((heads, 1, rows), f32),
            pltpu.VMEM((CHUNK, CHUNK), f32),
            pltpu.VMEM((width, rows), f32),
            pltpu.VMEM((whole, width), f32),
            pltpu.VMEM((whole, width), f32),
        ],
        compiler_params=pltpu.CompilerParams(vmem_limit_bytes=56 * MIB),
        cost_estimate=pl.CostEstimate(
            flops=10 * rows * LONGEST * width,
            bytes_accessed=2 * (4 * rows + 5 * LONGEST) * width,
            transcendentals=rows * LONGEST * heads,
        ),
        name="attend_back",
    )(bounds, q, q_t, k, k_t, v, grad, context, lse, span, cosine, sine)


def collect_kernel(
    bounds, low_t_ref, dq_ref, dk_ref, dv_ref, w_ref, part_ref, own_ref, dw_ref, dw_acc, *, last_bound
):
    rows, width = dq_ref.shape
    whole = dk_ref.shape[0]
    own_first = (whole - rows) // 2 // CHUNK
    w_q, w_k, w_v = (slice(i * width, (i + 1) * width) for i in range(3))
    low_own = low_t_ref[:, own_first * CHUNK : own_first * CHUNK + rows]
    dw_ref[:, w_q] = dot_nn(low_own, dq_ref[...]).astype(bf16)
    dw_acc[...] = jnp.zeros_like(dw_acc)
    part_ref[...] = jnp.zeros_like(part_ref)

    def add(keys):
        dk, dv = dk_ref[keys, :], dv_ref[keys, :]
        turned = low_t_ref[:, keys]
        dw_acc[:, :width] += dot_nn(turned, dk)
        dw_acc[:, width:] += dot_nn(turned, dv)
        return dot_nt(dk, w_ref[:, w_k]) + dot_nt(dv, w_ref[:, w_v])

    @pl.loop(bounds[0], bounds[last_bound])
    def _(c):
        keys = pl.ds(pl.multiple_of(c * CHUNK, CHUNK), CHUNK)
        outside = (c < own_first) | (c >= own_first + rows // CHUNK)

        @pl.when(outside)
        def _():
            part_ref[keys, :] = add(keys).astype(bf16)

        @pl.when(~outside)
        def _():
            own = pl.ds(pl.multiple_of((c - own_first) * CHUNK, CHUNK), CHUNK)
            own_ref[own, :] = add(keys) + dot_nt(dq_ref[own, :], w_ref[:, w_q])

    dw_ref[:, width:] = dw_acc[...].astype(bf16)


def collect(bounds, low_t, dq, dk, dv, weight):
    rows, width = dq.shape
    whole = dk.shape[0]
    spec = pl.BlockSpec(memory_space=pltpu.VMEM)
    return pl.pallas_call(
        functools.partial(collect_kernel, last_bound=bounds.shape[0] - 1),
        out_shape=[
            jax.ShapeDtypeStruct((whole, width), bf16),
            jax.ShapeDtypeStruct((rows, width), f32),
            jax.ShapeDtypeStruct(weight.shape, bf16),
        ],
        in_specs=[pl.BlockSpec(memory_space=pltpu.SMEM)] + [spec] * 5,
        out_specs=[spec] * 3,
        scratch_shapes=[pltpu.VMEM((width, 2 * width), f32)],
        compiler_params=pltpu.CompilerParams(vmem_limit_bytes=44 * MIB),
        cost_estimate=pl.CostEstimate(
            flops=4 * width * width * (rows + 2 * (rows + LONGEST)),
            bytes_accessed=2 * width * (8 * width + 6 * rows),
            transcendentals=0,
        ),
        name="collect",
    )(bounds, low_t, dq, dk, dv, weight)


def halve(value, axis, bit):
    count = lax.axis_size("dp")
    mine = (lax.axis_index("dp") >> bit) & 1
    size = value.shape[axis] // 2
    keep = lax.dynamic_slice_in_dim(value, mine * size, size, axis)
    send = lax.dynamic_slice_in_dim(value, (1 - mine) * size, size, axis)
    got = lax.ppermute(send, "dp", [(i, i ^ (1 << bit)) for i in range(count)])
    return (keep.astype(f32) + got.astype(f32)).astype(bf16)


def unhalve(value, axis, bit):
    count = lax.axis_size("dp")
    mine = (lax.axis_index("dp") >> bit) & 1
    got = lax.ppermute(value, "dp", [(i, i ^ (1 << bit)) for i in range(count)])
    first = jnp.where(mine == 0, value, got)
    second = jnp.where(mine == 0, got, value)
    return jnp.concatenate([first, second], axis=axis)


def reduce_grad(grad, flip):
    groups = lax.axis_size("seq")
    me = lax.axis_index("seq")
    bits = list(range(lax.axis_size("dp").bit_length() - 1))
    if flip:
        bits = bits[:1] + bits[:0:-1]
    stages = [(bit, 2 if at == 0 else 1) for at, bit in enumerate(bits)]
    value = grad.reshape(groups, grad.shape[0] // groups, grad.shape[1])
    for bit, axis in stages:
        value = halve(value, axis, bit)
    total = lax.dynamic_index_in_dim(value, me, 0, keepdims=False).astype(f32)
    for step in range(1, groups):
        send = lax.dynamic_index_in_dim(value, (me + step) % groups, 0, keepdims=False)
        total = total + lax.ppermute(
            send, "seq", [(i, (i + step) % groups) for i in range(groups)]
        ).astype(f32)
    value = total.astype(bf16)
    for bit, axis in reversed(stages):
        value = unhalve(value, axis - 1, bit)
    return value.astype(f32)


def gain_grad(weight, weight_grad, gain):
    groups = lax.axis_size("seq")
    me = lax.axis_index("seq")
    rows = weight_grad.shape[0]
    own = lax.dynamic_slice_in_dim(weight, me * rows, rows, 0).astype(f32)
    own_gain = lax.dynamic_slice_in_dim(gain, me * rows, rows, 0)
    del groups
    return jnp.sum(own * weight_grad, axis=1) / own_gain


def local(
    tokens,
    segment_ids,
    first_gain,
    qkv_weight,
    out_weight,
    second_gain,
    in_weight,
    down_weight,
    cotangent,
):
    groups = lax.axis_size("seq")
    me = lax.axis_index("seq")
    rows, width = tokens.shape[1:]
    reach = min(groups - 1, -(-(LONGEST - 1) // rows))
    blocks = 2 * reach + 1
    window = blocks * rows
    up = [(i, i + 1) for i in range(groups - 1)]
    down = [(i + 1, i) for i in range(groups - 1)]

    around = {0: tokens[0]}
    for step in range(1, reach + 1):
        around[-step] = lax.ppermute(around[1 - step], "seq", up)
        around[step] = lax.ppermute(around[step - 1], "seq", down)

    segments = segment_ids[0]
    base = (me - reach) * rows
    near = lax.dynamic_slice_in_dim(
        jnp.pad(segments, (reach * rows, reach * rows), constant_values=-1), me * rows, window
    )
    start = sum(
        jnp.where(near == doc, jnp.sum((segments < doc).astype(jnp.int32)), 0)
        for doc in range(DOCS)
    )
    stop = sum(
        jnp.where(near == doc, jnp.sum((segments <= doc).astype(jnp.int32)), 0)
        for doc in range(DOCS)
    )
    offsets = (base + jnp.arange(window, dtype=jnp.int32) - start).astype(f32)
    freqs = jnp.exp(
        jnp.arange(HEAD_DIM // 2, dtype=f32) * (-2.0 * math.log(rope_base) / HEAD_DIM)
    )
    angles = offsets[:, None] * jnp.tile(freqs, 2 * LANES // HEAD_DIM)[None, :]
    sign = jnp.where(jnp.arange(LANES) % HEAD_DIM < HEAD_DIM // 2, -1.0, 1.0)
    cosine, sine = jnp.cos(angles), jnp.sin(angles) * sign[None, :]
    own = slice(reach * rows, (reach + 1) * rows)
    span = jnp.stack([start[own] - base, stop[own] - base])
    bounds = jnp.stack(
        [span[0, ::CHUNK] // CHUNK, (span[1, CHUNK - 1 :: CHUNK] + CHUNK - 1) // CHUNK], axis=1
    ).reshape(-1)

    gain = first_gain[None, :]
    low, low_t, k, k_t, v, q, q_t = project(
        bounds, around[0], gain, qkv_weight, cosine, sine, reach, blocks
    )
    held = (low, low_t, k, k_t, v)
    for step in range(1, reach + 1):
        for at in (-step, step):
            held = project(
                bounds, around[at], gain, qkv_weight, cosine, sine, reach + at, blocks, held
            )
    low, low_t, k, k_t, v = held
    context, lse = attend(
        bounds, q, k, v, near[own][:, None], near.reshape(window // CHUNK, 1, CHUNK)
    )

    inputs = tokens[0].astype(f32)
    residual = inputs + jnp.dot(context, out_weight, preferred_element_type=f32)
    normed_second, scale_second = normalize(residual)
    lowered_second = (normed_second * second_gain).astype(bf16)
    gate_up = jnp.dot(lowered_second, in_weight, preferred_element_type=f32)
    width_ff = gate_up.shape[1] // 2
    gate, upper = gate_up[:, :width_ff], gate_up[:, width_ff:]
    erf_term = 0.5 * (1.0 + lax.erf(gate * (1.0 / math.sqrt(2.0))))
    activated = gate * erf_term
    hidden = (activated * upper).astype(bf16)
    output = (residual + jnp.dot(hidden, down_weight, preferred_element_type=f32)).astype(bf16)

    grad_out = cotangent[0]
    down_weight_grad = jnp.einsum("tf,td->fd", hidden, grad_out, preferred_element_type=f32)
    hidden_grad = jnp.einsum("td,fd->tf", grad_out, down_weight, preferred_element_type=f32)
    gelu_slope = erf_term + gate * jnp.exp(-0.5 * gate * gate) * (1.0 / math.sqrt(2.0 * math.pi))
    gate_up_grad = jnp.concatenate(
        [hidden_grad * upper * gelu_slope, hidden_grad * activated], axis=1
    ).astype(bf16)
    in_weight_grad = jnp.einsum(
        "td,tf->df", lowered_second, gate_up_grad, preferred_element_type=f32
    )
    second_norm_grad = jnp.einsum(
        "tf,df->td", gate_up_grad, in_weight, preferred_element_type=f32
    )
    residual_grad = grad_out.astype(f32) + normalize_back(
        second_norm_grad * second_gain, normed_second, scale_second
    )
    branch_grad = residual_grad.astype(bf16)
    out_weight_grad = jnp.einsum("tc,td->cd", context, branch_grad, preferred_element_type=f32)
    context_grad = jnp.einsum(
        "td,cd->tc", branch_grad, out_weight, preferred_element_type=f32
    ).astype(bf16)

    down_weight_grad = reduce_grad(down_weight_grad.astype(bf16), True)
    in_weight_grad = reduce_grad(in_weight_grad.astype(bf16), False)
    out_weight_grad = reduce_grad(out_weight_grad.astype(bf16), True)
    second_gain_grad = gain_grad(in_weight, in_weight_grad, second_gain)

    heads = width // HEAD_DIM
    dq, dk, dv = attend_back(
        bounds,
        q,
        q_t,
        k,
        k_t,
        v,
        context_grad,
        context,
        lse[:heads].reshape(heads, 1, rows),
        span,
        cosine,
        sine,
        reach * rows,
    )
    part, first_norm_grad, qkv_weight_grad = collect(bounds, low_t, dq, dk, dv, qkv_weight)

    def share(at):
        return part[(reach + at) * rows : (reach + at + 1) * rows]

    upward, downward = share(reach), share(-reach)
    for step in range(reach - 1, -1, -1):
        upward = lax.ppermute(upward, "seq", up)
        downward = lax.ppermute(downward, "seq", down)
        if step:
            upward = (share(step).astype(f32) + upward.astype(f32)).astype(bf16)
            downward = (share(-step).astype(f32) + downward.astype(f32)).astype(bf16)
    first_norm_grad = first_norm_grad + upward.astype(f32) + downward.astype(f32)

    qkv_weight_grad = reduce_grad(qkv_weight_grad, False)
    first_gain_grad = gain_grad(qkv_weight, qkv_weight_grad, first_gain)
    normed_first, scale_first = normalize(inputs)
    input_grad = (
        residual_grad + normalize_back(first_norm_grad * first_gain, normed_first, scale_first)
    ).astype(bf16)
    return (
        output[None],
        input_grad[None],
        qkv_weight_grad,
        out_weight_grad,
        in_weight_grad,
        down_weight_grad,
        first_gain_grad,
        second_gain_grad,
    )


def solution(mesh):
    in_specs = (
        P("dp", "seq", None),
        P("dp", None),
        P(),
        P(),
        P(),
        P(),
        P(),
        P(),
        P("dp", "seq", None),
    )
    out_specs = (
        P("dp", "seq", None),
        P("dp", "seq", None),
        P("seq", None),
        P("seq", None),
        P("seq", None),
        P("seq", None),
        P("seq"),
        P("seq"),
    )
    return jax.shard_map(local, mesh=mesh, in_specs=in_specs, out_specs=out_specs, check_vma=False)
```
